32 devices in a mesh: blk: 8 (over z, y), smp: 4 (over x, core).
Axes of the slice: x: 2, y: 2, z: 4, core: 2. Of those that a mesh axis runs over, the one named last changes fastest.
Arguments:
- forward_samples: bfloat16 [256, 65536], P('smp', 'blk'), may hold values from -0.375 to 0.375
- adjoint_samples: bfloat16 [256, 16384], P('smp', 'blk'), may hold values from -0.125 to 0.125
- probe_values: bfloat16 [16384, 192], P('blk'), may hold values from -6 to 6
- owners: int32 [16384, 1], P('blk'), may hold values from 0 to 7; in each aligned block of 2048 rows (0 to 2047, 2048 to 4095, ...) at most 512 rows name the same one
- block_ranks: int32 [8], P('blk'), may hold values from 64 to 256
- twiddle: float32 [2, 65536], P(None, 'blk'), may hold values from -1.2 to 1.2
Outputs:
- applied: bfloat16 [192, 65536], P('smp', 'blk')
The draws below stay inside these ranges and needn't reach their ends.
Inputs may be any that keep to these rules, and one draw needn't show every extreme that they name: `owners`: in the rows of one block index no owner block is named more than 512 times.
All inputs are finite; a program needn't handle non-finite values.
Results may differ from the reference program's by a relative error of at most 0.005.
Values may be sent and summed in bfloat16 or wider, within the bound.
A program may use at most 64 MiB of HBM per device.

```python
import math
import jax
import jax.numpy as jnp
import numpy as np
from jax import lax

SAMPLES = 256
BOX = 8192
VECTORS = 192
ADJ_ROWS = 2048
LEVELS = 2
BLOCKS = 8
CAPACITY = 512
N_BLK = 8


def with_ends(array, own_key, smallest, largest):
    spot = [jax.random.randint(jax.random.fold_in(own_key, axis), (), 0, length) for axis, length in enumerate(array.shape)]
    longest = array.shape.index(max(array.shape))
    beside = spot[:longest] + [(spot[longest] + 1) % array.shape[longest]] + spot[longest + 1:]
    return array.at[tuple(spot)].set(smallest).at[tuple(beside)].set(largest)


def block_levels(rng, shape, pieces, least, high):
    loudness, own = 1.0, jax.random.fold_in(rng, 6)
    for position, parts in pieces:
        steps = jnp.exp(jax.random.uniform(jax.random.fold_in(own, position), (parts,), jnp.float32, least / len(pieces), high / len(pieces)))
        loudness = loudness * jnp.repeat(steps, shape[position] // parts).reshape([-1 if axis == position else 1 for axis in range(len(shape))])
    return loudness


def shared_out(key, own, number, rows, amount, top, limit, lean):
    ranking = jax.random.permutation(key, amount)
    crowded, common = load_shares(amount, rows * top, limit, lean, True), load_shares(amount, rows * top, limit, lean, False)
    places = jnp.arange(amount)

    def named(lengths, rotation):
        used = int((lengths > 0).sum())
        fixed = max(1, used // 4)
        moved = fixed + (places - fixed + rotation * (used - fixed)) % max(1, amount - fixed)
        return jnp.zeros((amount,), jnp.int32).at[ranking[jnp.where(places < fixed, places, moved)]].set(jnp.asarray(lengths, jnp.int32))

    lengths = jnp.where(number % 4 == 0, named(crowded, number // 4), named(common, number - number // 4 - 1))
    mixed = jax.random.permutation(jax.random.fold_in(own, 3), amount)
    source_of, sink = mixed[0:amount // 2 * 2:2], mixed[1:amount // 2 * 2:2]
    margin = jnp.minimum(lengths[source_of] - 1, limit - lengths[sink]) // 2
    margin = jnp.where((source_of == ranking[0]) | (sink == ranking[0]) | (lengths[sink] == 0), 0, jnp.maximum(margin, 0))
    moved = jax.random.randint(jax.random.fold_in(own, 4), (amount // 2,), 0, 1 << 20) % (margin + 1)
    lengths = lengths.at[source_of].add(-moved).at[sink].add(moved)
    members = jnp.searchsorted(jnp.cumsum(lengths), jnp.arange(rows * top), side="right").astype(jnp.int32)
    listing = members.reshape(top, rows).T
    listing = listing[jax.random.permutation(jax.random.fold_in(own, 1), rows)]
    rotation = jax.random.randint(jax.random.fold_in(own, 2), (rows, 1), 0, top)
    return jnp.take_along_axis(listing, (jnp.arange(top)[None, :] + rotation) % top, axis=1)


def load_shares(amount, total, reach, lean, full):
    weights = [(1 << 20) // math.isqrt(grade ** lean) + 1 for grade in range(1, amount + 1)]
    largest = reach if full else min(reach, max(-(-total // amount), total * weights[0] // sum(weights)))
    least = 1 if total - largest >= amount - 1 else 0
    holding, spare = [largest] + [least] * (amount - 1), total - largest - least * (amount - 1)
    while spare > 0:
        movable = [i for i in range(1, amount) if holding[i] < largest] or [i for i in range(1, amount) if holding[i] < reach]
        mass, budget = sum([weights[i] for i in movable]), spare
        for i in movable:
            extra = min(reach - holding[i], max(1, budget * weights[i] // mass), spare)
            holding[i] = holding[i] + extra
            spare = spare - extra
    return np.array(holding)


def gaussian(key, shape, scale, reach, cuts=(), kind=jnp.bfloat16):
    values = jax.random.normal(key, shape, jnp.float32) * scale
    if len(cuts) > 0:
        values = block_levels(key, shape, cuts, -0.22, 0.18) * values
    return jnp.clip(values, min=-reach, max=reach).astype(kind)


def setup_inputs(seed: int = 0) -> dict:
    streams_of = jax.random.split(jax.random.key(seed), 7)
    forward_samples = gaussian(streams_of[0], (SAMPLES, BLOCKS * BOX), SAMPLES ** -0.5, 0.375, ((0, 4), (1, 8)))
    adjoint_samples = gaussian(streams_of[1], (SAMPLES, BLOCKS * ADJ_ROWS), ADJ_ROWS ** -0.5, 0.125, ((0, 4), (1, 8)))
    probe_values = gaussian(streams_of[2], (BLOCKS * ADJ_ROWS, VECTORS), 1.0, 6.0, ((0, 8),))
    owners_keys = jax.random.split(jax.random.fold_in(streams_of[3], 1), (BLOCKS * ADJ_ROWS) // ADJ_ROWS)
    owners_turns = jax.random.permutation(jax.random.fold_in(streams_of[3], 3), (BLOCKS * ADJ_ROWS) // ADJ_ROWS)
    owners = jax.vmap(lambda own, number: shared_out(jax.random.fold_in(streams_of[3], 2), own, number, ADJ_ROWS, BLOCKS, 1, CAPACITY, 2))(owners_keys, owners_turns).reshape((BLOCKS * ADJ_ROWS, 1))
    block_ranks = with_ends(jax.random.randint(streams_of[4], (BLOCKS,), SAMPLES // 4, SAMPLES + 1), jax.random.fold_in(streams_of[4], 1), SAMPLES // 4, SAMPLES).astype(jnp.int32)
    twiddle = jnp.clip(jax.random.uniform(streams_of[5], (LEVELS, BLOCKS * BOX), jnp.float32, -1.2, 1.2) * block_levels(streams_of[5], (LEVELS, BLOCKS * BOX), ((1, 8),), -0.4, 0.0), -1.2, 1.2)
    return dict(forward_samples=forward_samples, adjoint_samples=adjoint_samples, probe_values=probe_values, owners=owners, block_ranks=block_ranks, twiddle=twiddle)


def reference(forward_samples, adjoint_samples, probe_values, owners, block_ranks, twiddle):
    blocks = N_BLK
    owner_ids = owners[:, 0].astype(jnp.int32)
    per_block = ADJ_ROWS
    adj_rows = adjoint_samples.astype(jnp.float32).T.reshape(blocks, per_block, SAMPLES)
    probe_rows = probe_values.astype(jnp.float32).reshape(blocks, per_block, VECTORS)
    owner_rows = owner_ids.reshape(blocks, per_block)

    def accumulate(carry, items):
        adj_part, probe_part, owner_part = items
        outer = adj_part[:, :, None] * probe_part[:, None, :]
        return carry + jax.ops.segment_sum(outer, owner_part, num_segments=blocks), None

    start_sum = jnp.zeros((blocks, SAMPLES, VECTORS), jnp.float32)
    coeffs, unused = lax.scan(accumulate, start_sum, (adj_rows, probe_rows, owner_rows))
    keep_mask = (jnp.arange(SAMPLES, dtype=jnp.int32)[None, :] < block_ranks[:, None]).astype(jnp.float32)
    weights = lax.optimization_barrier((coeffs * keep_mask[:, :, None]).astype(jnp.bfloat16)).astype(jnp.float32)
    forward_grid = forward_samples.astype(jnp.float32).reshape(SAMPLES, blocks, BOX)
    field = jnp.einsum('bsv,sbm->vbm', weights, forward_grid)
    factors = twiddle.astype(jnp.float32).reshape(LEVELS, blocks, BOX)
    for level_index in range(LEVELS):
        distance = blocks // (2 ** (level_index + 1))
        partner_ids = jnp.bitwise_xor(jnp.arange(blocks, dtype=jnp.int32), distance)
        partner = jnp.take(field, partner_ids, axis=1)
        field = field + factors[level_index][None, :, :] * partner
    return field.reshape(VECTORS, blocks * BOX).astype(jnp.bfloat16)
```

```python
import functools

import jax
import jax.numpy as jnp
from jax import lax
from jax.experimental import pallas as pl
from jax.experimental.pallas import tpu as pltpu
from jax.sharding import PartitionSpec as P

CHUNKS = 2
STAGES = (2, 3, 4)


def kernel(
    blocks, smp, fwd, adj_in, probe_in, tw_in, owners_in, ranks, out,
    adj, probe, owners, part, part_in, piece, piece_in, across, across_in, gathered, left, limits,
    xbuf, twbuf, obuf,
    load_sem, part_send, part_recv, piece_send, piece_recv,
    col_send, col_recv, limit_send, limit_recv, x_send, x_recv, x_own,
    tw_send, tw_recv, tw_own, o_send, o_recv, o_own,
):
    levels = tw_in.shape[0]
    group = 2 ** levels
    low_count = blocks // group
    samples = fwd.shape[0]
    vectors = probe_in.shape[0]
    vlocal = vectors // smp
    span = fwd.shape[1] // (group * smp)
    chunks, width = xbuf.shape[0], xbuf.shape[2]
    depth = group * samples
    blk, j = lax.axis_index("blk"), lax.axis_index("smp")
    h, low = blk // low_count, blk % low_count
    rank = h * smp + j
    odd = h % 2
    pair = h + 1 - 2 * odd

    def up_h(d):
        return (h + d) % group

    def up_j(d):
        return (j + d) % smp

    def dev(hh, ll, jj):
        return {"blk": hh * low_count + ll, "smp": jj}

    def remote(src, dst, send, recv, where):
        return pltpu.make_async_remote_copy(
            src_ref=src, dst_ref=dst, send_sem=send, recv_sem=recv,
            device_id=where, device_id_type=pl.DeviceIdType.MESH,
        )

    shifts = [(dh, dj) for dh in range(group) for dj in range(smp)]
    far = [s for s in shifts if s != (0, 0)]
    far.sort(key=lambda s: (-min(s[0], group - s[0]), s[0], s[1]))

    loads = [
        pltpu.make_async_copy(src, dst, load_sem.at[i])
        for i, (src, dst) in enumerate(((owners_in, owners), (adj_in, adj), (probe_in, probe)))
    ]
    for c in loads:
        c.start()

    barrier = pltpu.get_barrier_semaphore()
    for dh, dj in far:
        pl.semaphore_signal(
            barrier, inc=1, device_id=dev(up_h(dh), low, up_j(dj)),
            device_id_type=pl.DeviceIdType.MESH,
        )
    for d in range(1, low_count):
        pl.semaphore_signal(
            barrier, inc=1, device_id=dev(h, (low + d) % low_count, j),
            device_id_type=pl.DeviceIdType.MESH,
        )
    def aligned(start, size):
        return pl.ds(pl.multiple_of(start, size), size)

    for c in loads:
        c.wait()

    def partial_sums(lo):
        stacked = jnp.concatenate(
            [
                adj[...] * (owners[...] == hh * low_count + lo).astype(jnp.bfloat16)
                for hh in range(group)
            ],
            axis=0,
        )
        part[lo] = lax.dot_general(
            probe[...], stacked, (((1,), (1,)), ((), ())), preferred_element_type=jnp.float32
        )

    if low_count > 2:
        lax.fori_loop(0, low_count, lambda lo, c: (partial_sums(lo), c)[1], 0)
    else:
        for lo in range(low_count):
            partial_sums(lo)
    limits[h] = jnp.full(limits.shape[1:], ranks[0].astype(jnp.float32))

    pl.semaphore_wait(barrier, len(far) + low_count - 1)

    def part_copy(d):
        lo = (low + d) % low_count
        return remote(
            part.at[lo], part_in.at[d], part_send.at[d], part_recv.at[d], dev(h, lo, j)
        )

    def send_part(d, carry):
        part_copy(d).start()
        return carry

    if low_count > 1:
        lax.fori_loop(1, low_count, send_part, 0)

    def x_copy(k, dh, dj):
        to = up_h(dh) * smp + up_j(dj)
        src = fwd.at[:, aligned(to * span + k * width, width)]
        dst = xbuf.at[k, aligned(j * depth + h * samples, samples), :]
        if (dh, dj) == (0, 0):
            return pltpu.make_async_copy(src, dst, x_own.at[k])
        index = dh * smp + dj
        return remote(
            src, dst, x_send.at[k, index], x_recv.at[k, index], dev(up_h(dh), low, up_j(dj))
        )

    turns = sorted(range(group), key=lambda d: (d == 0, abs(2 * d - group)))
    x_units = [(k, dh) for k in range(chunks) for dh in turns]
    x_copies = {k: [] for k in range(chunks)}

    def send_x(first, last):
        for k, dh in x_units[first:last]:
            for dj in range(smp):
                c = x_copy(k, dh, dj)
                c.start()
                x_copies[k].append(c)

    send_x(0, STAGES[0])
    tw_copies = []
    for dh in range(group):
        src = tw_in.at[:, aligned((up_h(dh) * smp + j) * span, span)]
        dst = twbuf.at[h]
        if dh == 0:
            tw_copies.append(pltpu.make_async_copy(src, dst, tw_own))
        else:
            tw_copies.append(
                remote(src, dst, tw_send.at[dh], tw_recv.at[dh], dev(up_h(dh), low, j))
            )
            tw_copies.append(
                remote(
                    limits.at[h], limits.at[h], limit_send.at[dh], limit_recv.at[dh],
                    dev(up_h(dh), low, j),
                )
            )
    for c in tw_copies:
        c.start()

    total = part.at[low]

    def add_part(d, carry):
        part_copy(d).wait()
        total[...] += part_in[d]
        return carry

    if low_count > 1:
        lax.fori_loop(1, low_count, add_part, 0)

    half = vectors // 2
    mine, theirs = aligned(odd * half, half), aligned((1 - odd) * half, half)
    piece[...] = total[theirs, :].astype(jnp.bfloat16)
    pair_copy = remote(
        piece, piece_in, piece_send.at[0], piece_recv.at[0], dev(pair, low, j)
    )
    pair_copy.start()
    send_x(STAGES[0], STAGES[1])
    pair_copy.wait()
    coeffs = total[mine, :] + piece_in[...].astype(jnp.float32)
    across[...] = coeffs.astype(jnp.bfloat16)
    across_copy = remote(
        across, across_in, piece_send.at[1], piece_recv.at[1], dev(up_h(group // 2), low, j)
    )
    across_copy.start()
    send_x(STAGES[1], STAGES[2])
    across_copy.wait()
    coeffs += across_in[...].astype(jnp.float32)
    gathered[j, mine, :] = coeffs.astype(jnp.bfloat16)
    own = gathered.at[j, mine, :]
    col_copies = {
        (dp, dj): remote(
            own, own, col_send.at[dp, dj], col_recv.at[dp, dj],
            dev((h, pair)[dp], low, up_j(dj)),
        )
        for dj in range(smp) for dp in range(2) if (dp, dj) != (0, 0)
    }
    for c in col_copies.values():
        c.start()
    send_x(STAGES[2], len(x_units))
    for c in tw_copies:
        c.wait()
    lane = lax.broadcasted_iota(jnp.int32, (1, depth), 1)

    def spread(jj):
        number = (jj * samples + lane % samples).astype(jnp.float32)
        for hh in range(group):
            keep = (lane // samples == hh) & (number < limits[hh, 0:1, 0:1])
            left[hh * vectors : (hh + 1) * vectors, aligned(jj * depth, depth)] = (
                gathered[jj] * keep.astype(jnp.bfloat16)
            )

    for dj in range(smp):
        for dp in range(2):
            if (dp, dj) in col_copies:
                col_copies[dp, dj].wait()
        spread((j + smp - dj) % smp)

    o_copies = []
    for k in range(chunks):
        for c in x_copies[k]:
            c.wait()
        product = jnp.dot(left[...], xbuf[k], preferred_element_type=jnp.float32)
        field = [product[hh * vectors : (hh + 1) * vectors] for hh in range(group)]
        for level in range(levels):
            distance = group >> (level + 1)
            field = [
                field[hh]
                + twbuf[hh, level : level + 1, k * width : (k + 1) * width]
                * field[hh ^ distance]
                for hh in range(group)
            ]
        for hh in range(group):
            obuf[k, hh] = field[hh].astype(jnp.bfloat16)
        cols = aligned(rank * span + k * width, width)
        for dh, dj in far + [(0, 0)]:
            src = obuf.at[k, up_h(dh), aligned(up_j(dj) * vlocal, vlocal), :]
            dst = out.at[:, cols]
            if (dh, dj) == (0, 0):
                c = pltpu.make_async_copy(src, dst, o_own.at[k])
            else:
                index = dh * smp + dj
                c = remote(
                    src, dst, o_send.at[k, index], o_recv.at[k, index],
                    dev(up_h(dh), low, up_j(dj)),
                )
            c.start()
            o_copies.append(c)
    for c in o_copies:
        c.wait()


def body(blocks, smp, fwd, adj, probe, owners, ranks, twiddle):
    samples, box = fwd.shape
    rows, vectors = probe.shape
    levels = twiddle.shape[0]
    group = 2 ** levels
    low_count = blocks // group
    peers = group * smp
    span = box // peers
    chunks = CHUNKS
    width = span // chunks
    depth = group * samples
    dma = pltpu.SemaphoreType.DMA
    hbm = pl.BlockSpec(memory_space=pltpu.HBM)
    return pl.pallas_call(
        functools.partial(kernel, blocks, smp),
        out_shape=pltpu.VMEM((vectors // smp, box), jnp.bfloat16),
        in_specs=[
            hbm, hbm, hbm, hbm, hbm,
            pl.BlockSpec(memory_space=pltpu.SMEM),
        ],
        out_specs=pl.BlockSpec(memory_space=pltpu.VMEM),
        scratch_shapes=[
            pltpu.VMEM(adj.shape, jnp.bfloat16),
            pltpu.VMEM((vectors, rows), jnp.bfloat16),
            pltpu.VMEM((1, rows), jnp.int32),
            pltpu.VMEM((low_count, vectors, depth), jnp.float32),
            pltpu.VMEM((low_count, vectors, depth), jnp.float32),
            pltpu.VMEM((vectors // 2, depth), jnp.bfloat16),
            pltpu.VMEM((vectors // 2, depth), jnp.bfloat16),
            pltpu.VMEM((vectors // 2, depth), jnp.bfloat16),
            pltpu.VMEM((vectors // 2, depth), jnp.bfloat16),
            pltpu.VMEM((smp, vectors, depth), jnp.bfloat16),
            pltpu.VMEM((group * vectors, smp * depth), jnp.bfloat16),
            pltpu.VMEM((group, 8, 128), jnp.float32),
            pltpu.VMEM((chunks, smp * depth, width), jnp.bfloat16),
            pltpu.VMEM((group, levels, span), jnp.float32),
            pltpu.VMEM((chunks, group, vectors, width), jnp.bfloat16),
            dma((3,)),
            dma((low_count,)), dma((low_count,)),
            dma((2,)), dma((2,)),
            dma((2, smp)), dma((2, smp)),
            dma((group,)), dma((group,)),
            dma((chunks, peers)), dma((chunks, peers)), dma((chunks,)),
            dma((group,)), dma((group,)), dma,
            dma((chunks, peers)), dma((chunks, peers)), dma((chunks,)),
        ],
        compiler_params=pltpu.CompilerParams(
            collective_id=0, has_side_effects=True, vmem_limit_bytes=66000000
        ),
        name="butterfly",
    )(fwd, adj, probe.T, twiddle, owners.reshape(1, rows), ranks)


def solution(mesh):
    in_specs = (
        P("smp", "blk"),
        P("smp", "blk"),
        P("blk", None),
        P("blk", None),
        P("blk"),
        P(None, "blk"),
    )
    return jax.shard_map(
        functools.partial(body, mesh.shape["blk"], mesh.shape["smp"]),
        mesh=mesh, in_specs=in_specs, out_specs=P("smp", "blk"), check_vma=False,
    )
```

```python
import functools

import jax
import jax.numpy as jnp
from jax import lax
from jax.experimental import pallas as pl
from jax.experimental.pallas import tpu as pltpu
from jax.sharding import PartitionSpec as P

WIDTHS = (2, 2)
PLAN = (
    ((0, 2, 0), (0, 2, 2)),
    ((0, 3, 0), (0, 3, 2)),
    ((0, 1, 0), (0, 1, 2), (0, 0, 0), (0, 0, 2)),
    ((1, 2, 0), (1, 2, 2), (1, 1, 0), (1, 1, 2), (1, 0, 0), (1, 0, 2), (1, 3, 0), (1, 3, 2)),
)


def kernel(
    blocks, smp, widths, fwd, adj_in, probe_in, tw_in, owners_in, ranks, out,
    adj, probe, owners, part, part_out, part_in, piece, piece_in, across, across_in, gathered, left, limits,
    xbuf, twbuf, obuf, ready,
    load_sem, part_send, part_recv, piece_send, piece_recv,
    col_send, col_recv, limit_send, limit_recv, x_send, x_recv, x_own,
    tw_send, tw_recv, tw_own, o_send, o_recv, o_own,
):
    levels = tw_in.shape[0]
    group = 2 ** levels
    half_group = group // 2
    low_count = blocks // group
    samples = fwd.shape[0]
    vectors = probe_in.shape[0]
    vlocal = vectors // smp
    span = xbuf.shape[1]
    starts = [sum(widths[:k]) for k in range(len(widths))]
    chunks = len(widths)
    depth = group * samples
    blk, j = lax.axis_index("blk"), lax.axis_index("smp")
    h, low = blk // low_count, blk % low_count
    rank = h * smp + j
    odd = h % 2
    pair = h + 1 - 2 * odd
    inner = ((h + 1) // 2) % 2 == 1

    def up_h(d):
        return (h + d) % group

    def flip(d):
        bits = [(h // 2 ** i) % 2 for i in range(levels)]
        return sum((1 - b if (d >> i) % 2 else b) * 2 ** i for i, b in enumerate(bits))

    def up_j(d):
        return (j + d) % smp

    def dev(hh, ll, jj):
        return {"blk": hh * low_count + ll, "smp": jj}

    def remote(src, dst, send, recv, where):
        return pltpu.make_async_remote_copy(
            src_ref=src, dst_ref=dst, send_sem=send, recv_sem=recv,
            device_id=where, device_id_type=pl.DeviceIdType.MESH,
        )

    shifts = [(dh, dj) for dh in range(group) for dj in range(smp)]
    far = [s for s in shifts if s != (0, 0)]
    far.sort(key=lambda s: (-min(s[0], group - s[0]), s[0], s[1]))

    loads = [
        pltpu.make_async_copy(src, dst, load_sem.at[i])
        for i, (src, dst) in enumerate(((owners_in, owners), (adj_in, adj), (probe_in, probe)))
    ]
    for c in loads:
        c.start()

    barrier = pltpu.get_barrier_semaphore()
    other = [(1 - h // half_group) * half_group + i for i in range(half_group)]
    for hh in other:
        for dj in range(smp):
            pl.semaphore_signal(
                barrier, inc=1, device_id=dev(hh, low, up_j(dj)),
                device_id_type=pl.DeviceIdType.MESH,
            )
    for d in range(1, low_count):
        pl.semaphore_signal(
            barrier, inc=1, device_id=dev(h, (low + d) % low_count, j),
            device_id_type=pl.DeviceIdType.MESH,
        )
    def aligned(start, size):
        return pl.ds(pl.multiple_of(start, size), size)

    def x_copy(k, d, dj):
        to = up_h(d) * smp + up_j(dj)
        src = fwd.at[:, pl.ds(pl.multiple_of(to * span + starts[k], 128), widths[k])]
        dst = xbuf.at[
            aligned(j * depth + h * samples, samples), starts[k] : starts[k] + widths[k]
        ]
        if (d, dj) == (0, 0):
            return pltpu.make_async_copy(src, dst, x_own.at[k])
        return remote(
            src, dst, x_send.at[k, d, dj], x_recv.at[k, d, dj], dev(up_h(d), low, up_j(dj))
        )

    def send_x(stage):
        for k, d, half in PLAN[stage]:
            for dj in (half, half + 1):
                x_copy(k, d, dj).start()

    def enter():
        pl.semaphore_wait(barrier, half_group * smp + low_count - 1)
        pl.semaphore_signal(
            ready, inc=1, device_id=dev(up_h(half_group), low, j),
            device_id_type=pl.DeviceIdType.MESH,
        )
        send_x(0)

    pl.when(h >= half_group)(enter)
    for c in loads:
        c.wait()

    def partial_sums(lo):
        stacked = jnp.concatenate(
            [
                adj[...] * (owners[...] == hh * low_count + lo).astype(jnp.bfloat16)
                for hh in range(group)
            ],
            axis=0,
        )
        part[lo] = lax.dot_general(
            probe[...], stacked, (((1,), (1,)), ((), ())), preferred_element_type=jnp.float32
        )
        part_out[lo] = part[lo].astype(jnp.bfloat16)

    if low_count > 2:
        lax.fori_loop(0, low_count, lambda lo, c: (partial_sums(lo), c)[1], 0)
    else:
        for lo in range(low_count):
            partial_sums(lo)
    limits[h] = jnp.full(limits.shape[1:], ranks[0].astype(jnp.float32))


    pl.when(h < half_group)(enter)

    def part_copy(d):
        lo = (low + d) % low_count
        return remote(
            part_out.at[lo], part_in.at[d], part_send.at[d], part_recv.at[d], dev(h, lo, j)
        )

    def send_part(d, carry):
        part_copy(d).start()
        return carry

    if low_count > 1:
        lax.fori_loop(1, low_count, send_part, 0)


    total = part.at[low]

    def add_part(d, carry):
        part_copy(d).wait()
        total[...] += part_in[d].astype(jnp.float32)
        return carry

    if low_count > 1:
        lax.fori_loop(1, low_count, add_part, 0)

    half = vectors // 2
    mine, theirs = aligned(odd * half, half), aligned((1 - odd) * half, half)
    piece[...] = total[theirs, :].astype(jnp.bfloat16)
    pair_copy = remote(
        piece, piece_in, piece_send.at[0], piece_recv.at[0], dev(pair, low, j)
    )
    pl.semaphore_wait(ready, 1)
    pair_copy.start()
    tw_copies = []
    for dh in range(group):
        src = tw_in.at[:, aligned((up_h(dh) * smp + j) * span, span)]
        dst = twbuf.at[h]
        if dh == 0:
            tw_copies.append(pltpu.make_async_copy(src, dst, tw_own))
        else:
            tw_copies.append(
                remote(src, dst, tw_send.at[dh], tw_recv.at[dh], dev(up_h(dh), low, j))
            )
            tw_copies.append(
                remote(
                    limits.at[h], limits.at[h], limit_send.at[dh], limit_recv.at[dh],
                    dev(up_h(dh), low, j),
                )
            )
    for c in tw_copies:
        c.start()
    send_x(1)
    pair_copy.wait()
    coeffs = total[mine, :] + piece_in[...].astype(jnp.float32)
    across[...] = coeffs.astype(jnp.bfloat16)
    across_copy = remote(
        across, across_in, piece_send.at[1], piece_recv.at[1], dev(up_h(group // 2), low, j)
    )
    across_copy.start()
    send_x(2)
    across_copy.wait()
    coeffs += across_in[...].astype(jnp.float32)
    gathered[j, mine, :] = coeffs.astype(jnp.bfloat16)
    own = gathered.at[j, mine, :]
    col_copies = {
        (dp, dj): remote(
            own, own, col_send.at[dp, dj], col_recv.at[dp, dj],
            dev((h, pair)[dp], low, up_j(dj)),
        )
        for dj in range(smp) for dp in range(2) if (dp, dj) != (0, 0)
    }
    for c in col_copies.values():
        c.start()
    send_x(3)
    for c in tw_copies:
        c.wait()
    lane = lax.broadcasted_iota(jnp.int32, (1, depth), 1)

    def spread(jj):
        number = (jj * samples + lane % samples).astype(jnp.float32)
        for hh in range(group):
            keep = (lane // samples == hh) & (number < limits[hh, 0:1, 0:1])
            left[hh * vectors : (hh + 1) * vectors, aligned(jj * depth, depth)] = (
                gathered[jj] * keep.astype(jnp.bfloat16)
            )

    for dj in range(smp):
        for dp in range(2):
            if (dp, dj) in col_copies:
                col_copies[dp, dj].wait()
        spread((j + smp - dj) % smp)

    o_copies = []
    for k in range(chunks):
        for d, dj in far + [(0, 0)]:
            x_copy(k, d, dj).wait()
        now = slice(starts[k], starts[k] + widths[k])
        product = jnp.dot(left[...], xbuf[:, now], preferred_element_type=jnp.float32)
        field = [product[hh * vectors : (hh + 1) * vectors] for hh in range(group)]
        for level in range(levels):
            distance = group >> (level + 1)
            field = [
                field[hh]
                + twbuf[hh, level : level + 1, now]
                * field[hh ^ distance]
                for hh in range(group)
            ]
        for hh in range(group):
            obuf[hh, :, now] = field[hh].astype(jnp.bfloat16)
        cols = pl.ds(pl.multiple_of(rank * span + starts[k], 128), widths[k])
        for dh, dj in far + [(0, 0)]:
            src = obuf.at[up_h(dh), aligned(up_j(dj) * vlocal, vlocal), now]
            dst = out.at[:, cols]
            if (dh, dj) == (0, 0):
                c = pltpu.make_async_copy(src, dst, o_own.at[k])
            else:
                c = remote(
                    src, dst, o_send.at[k, dh, dj], o_recv.at[k, dh, dj],
                    dev(up_h(dh), low, up_j(dj)),
                )
            c.start()
            o_copies.append(c)
    for c in o_copies:
        c.wait()


def body(blocks, smp, fwd, adj, probe, owners, ranks, twiddle):
    samples, box = fwd.shape
    rows, vectors = probe.shape
    levels = twiddle.shape[0]
    group = 2 ** levels
    low_count = blocks // group
    peers = group * smp
    span = box // peers
    widths = tuple(span * w // sum(WIDTHS) for w in WIDTHS)
    chunks = len(widths)
    depth = group * samples
    dma = pltpu.SemaphoreType.DMA
    hbm = pl.BlockSpec(memory_space=pltpu.HBM)
    return pl.pallas_call(
        functools.partial(kernel, blocks, smp, widths),
        out_shape=pltpu.VMEM((vectors // smp, box), jnp.bfloat16),
        in_specs=[
            hbm, hbm, hbm, hbm, hbm,
            pl.BlockSpec(memory_space=pltpu.SMEM),
        ],
        out_specs=pl.BlockSpec(memory_space=pltpu.VMEM),
        scratch_shapes=[
            pltpu.VMEM(adj.shape, jnp.bfloat16),
            pltpu.VMEM((vectors, rows), jnp.bfloat16),
            pltpu.VMEM((1, rows), jnp.int32),
            pltpu.VMEM((low_count, vectors, depth), jnp.float32),
            pltpu.VMEM((low_count, vectors, depth), jnp.bfloat16),
            pltpu.VMEM((low_count, vectors, depth), jnp.bfloat16),
            pltpu.VMEM((vectors // 2, depth), jnp.bfloat16),
            pltpu.VMEM((vectors // 2, depth), jnp.bfloat16),
            pltpu.VMEM((vectors // 2, depth), jnp.bfloat16),
            pltpu.VMEM((vectors // 2, depth), jnp.bfloat16),
            pltpu.VMEM((smp, vectors, depth), jnp.bfloat16),
            pltpu.VMEM((group * vectors, smp * depth), jnp.bfloat16),
            pltpu.VMEM((group, 8, 128), jnp.float32),
            pltpu.VMEM((smp * depth, span), jnp.bfloat16),
            pltpu.VMEM((group, levels, span), jnp.float32),
            pltpu.VMEM((group, vectors, span), jnp.bfloat16),
            pltpu.SemaphoreType.REGULAR,
            dma((3,)),
            dma((low_count,)), dma((low_count,)),
            dma((2,)), dma((2,)),
            dma((2, smp)), dma((2, smp)),
            dma((group,)), dma((group,)),
            dma((chunks, group, smp)), dma((chunks, group, smp)), dma((chunks,)),
            dma((group,)), dma((group,)), dma,
            dma((chunks, group, smp)), dma((chunks, group, smp)), dma((chunks,)),
        ],
        compiler_params=pltpu.CompilerParams(
            collective_id=0, has_side_effects=True, vmem_limit_bytes=66000000
        ),
        name="butterfly",
    )(fwd, adj, probe.T, twiddle, owners.reshape(1, rows), ranks)


def solution(mesh):
    in_specs = (
        P("smp", "blk"),
        P("smp", "blk"),
        P("blk", None),
        P("blk", None),
        P("blk"),
        P(None, "blk"),
    )
    return jax.shard_map(
        functools.partial(body, mesh.shape["blk"], mesh.shape["smp"]),
        mesh=mesh, in_specs=in_specs, out_specs=P("smp", "blk"), check_vma=False,
    )
```

```python
import functools

import jax
import jax.numpy as jnp
from jax import lax
from jax.experimental import pallas as pl
from jax.experimental.pallas import tpu as pltpu
from jax.sharding import PartitionSpec as P

WIDTHS = (2, 2)


def kernel(
    blocks, smp, widths, fwd, adj_in, probe_in, tw_in, owners_in, ranks, out,
    adj, probe, owners, part, part_out, part_in, piece, piece_in, across, across_in, gathered, left, limits,
    xbuf, twbuf, obuf, ready,
    load_sem, part_send, part_recv, piece_send, piece_recv,
    col_send, col_recv, limit_send, limit_recv, x_send, x_recv, x_own,
    tw_send, tw_recv, tw_own, o_send, o_recv, o_own,
):
    levels = tw_in.shape[0]
    group = 2 ** levels
    half_group = group // 2
    low_count = blocks // group
    samples = fwd.shape[0]
    vectors = probe_in.shape[0]
    vlocal = vectors // smp
    span = xbuf.shape[1]
    starts = [sum(widths[:k]) for k in range(len(widths))]
    chunks = len(widths)
    depth = group * samples
    blk, j = lax.axis_index("blk"), lax.axis_index("smp")
    h, low = blk // low_count, blk % low_count
    rank = h * smp + j
    odd = h % 2
    pair = h + 1 - 2 * odd
    inner = ((h + 1) // 2) % 2 == 1

    def up_h(d):
        return (h + d) % group

    def flip(d):
        bits = [(h // 2 ** i) % 2 for i in range(levels)]
        return sum((1 - b if (d >> i) % 2 else b) * 2 ** i for i, b in enumerate(bits))

    def up_j(d):
        return (j + d) % smp

    def dev(hh, ll, jj):
        return {"blk": hh * low_count + ll, "smp": jj}

    def remote(src, dst, send, recv, where):
        return pltpu.make_async_remote_copy(
            src_ref=src, dst_ref=dst, send_sem=send, recv_sem=recv,
            device_id=where, device_id_type=pl.DeviceIdType.MESH,
        )

    shifts = [(dh, dj) for dh in range(group) for dj in range(smp)]
    far = [s for s in shifts if s != (0, 0)]
    far.sort(key=lambda s: (-min(s[0], group - s[0]), s[0], s[1]))
    turns = [*range(smp // 2, smp), *range(smp // 2 - 1, -1, -1)]
    out_order = [
        (d, i) for d in sorted(range(group), key=lambda d: (-min(d, group - d), d)) for i in turns
    ]

    loads = [
        pltpu.make_async_copy(src, dst, load_sem.at[i])
        for i, (src, dst) in enumerate(((owners_in, owners), (adj_in, adj), (probe_in, probe)))
    ]
    for c in loads:
        c.start()

    barrier = pltpu.get_barrier_semaphore()
    other = [(1 - h // half_group) * half_group + i for i in range(half_group)]
    for hh in other:
        for dj in range(smp):
            pl.semaphore_signal(
                barrier, inc=1, device_id=dev(hh, low, up_j(dj)),
                device_id_type=pl.DeviceIdType.MESH,
            )
    for d in range(1, low_count):
        pl.semaphore_signal(
            barrier, inc=1, device_id=dev(h, (low + d) % low_count, j),
            device_id_type=pl.DeviceIdType.MESH,
        )
    def aligned(start, size):
        return pl.ds(pl.multiple_of(start, size), size)

    def x_copy(k, d, dj):
        to = up_h(d) * smp + up_j(dj)
        src = fwd.at[:, pl.ds(pl.multiple_of(to * span + starts[k], 128), widths[k])]
        dst = xbuf.at[
            aligned(j * depth + h * samples, samples), starts[k] : starts[k] + widths[k]
        ]
        if (d, dj) == (0, 0):
            return pltpu.make_async_copy(src, dst, x_own.at[k])
        return remote(
            src, dst, x_send.at[k, d, dj], x_recv.at[k, d, dj], dev(up_h(d), low, up_j(dj))
        )

    plan = (
        [(0, half_group)],
        [(0, group - 1)],
        [(0, d) for d in range(1, group - 1) if d != half_group] + [(0, 0)],
        [
            (k, d)
            for k in range(1, chunks)
            for d in (*range(half_group, -1, -1), *range(half_group + 1, group))
        ],
    )

    def send_x(stage):
        for k, d in plan[stage]:
            for dj in range(smp):
                x_copy(k, d, dj).start()

    def enter():
        pl.semaphore_wait(barrier, half_group * smp + low_count - 1)
        pl.semaphore_signal(
            ready, inc=1, device_id=dev(up_h(half_group), low, j),
            device_id_type=pl.DeviceIdType.MESH,
        )
        send_x(0)

    pl.when(h >= half_group)(enter)
    for c in loads:
        c.wait()

    def partial_sums(lo):
        stacked = jnp.concatenate(
            [
                adj[...] * (owners[...] == hh * low_count + lo).astype(jnp.bfloat16)
                for hh in range(group)
            ],
            axis=0,
        )
        part[lo] = lax.dot_general(
            probe[...], stacked, (((1,), (1,)), ((), ())), preferred_element_type=jnp.float32
        )
        part_out[lo] = part[lo].astype(jnp.bfloat16)

    if low_count > 2:
        lax.fori_loop(0, low_count, lambda lo, c: (partial_sums(lo), c)[1], 0)
    else:
        for lo in range(low_count):
            partial_sums(lo)
    limits[h] = jnp.full(limits.shape[1:], ranks[0].astype(jnp.float32))


    pl.when(h < half_group)(enter)

    def part_copy(d):
        lo = (low + d) % low_count
        return remote(
            part_out.at[lo], part_in.at[d], part_send.at[d], part_recv.at[d], dev(h, lo, j)
        )

    def send_part(d, carry):
        part_copy(d).start()
        return carry

    if low_count > 1:
        lax.fori_loop(1, low_count, send_part, 0)


    total = part.at[low]

    def add_part(d, carry):
        part_copy(d).wait()
        total[...] += part_in[d].astype(jnp.float32)
        return carry

    if low_count > 1:
        lax.fori_loop(1, low_count, add_part, 0)

    half = vectors // 2
    mine, theirs = aligned(odd * half, half), aligned((1 - odd) * half, half)
    piece[...] = total[theirs, :].astype(jnp.bfloat16)
    pair_copy = remote(
        piece, piece_in, piece_send.at[0], piece_recv.at[0], dev(pair, low, j)
    )
    pl.semaphore_wait(ready, 1)
    pair_copy.start()
    tw_copies, limit_copies = [], []
    for dh in range(group):
        src = tw_in.at[:, aligned((up_h(dh) * smp + j) * span, span)]
        dst = twbuf.at[h]
        if dh == 0:
            tw_copies.append(pltpu.make_async_copy(src, dst, tw_own))
        else:
            tw_copies.append(
                remote(src, dst, tw_send.at[dh], tw_recv.at[dh], dev(up_h(dh), low, j))
            )
            limit_copies.append(
                remote(
                    limits.at[h], limits.at[h], limit_send.at[dh], limit_recv.at[dh],
                    dev(up_h(dh), low, j),
                )
            )
    for c in limit_copies + tw_copies:
        c.start()
    send_x(1)
    pair_copy.wait()
    coeffs = total[mine, :] + piece_in[...].astype(jnp.float32)
    across[...] = coeffs.astype(jnp.bfloat16)
    across_copy = remote(
        across, across_in, piece_send.at[1], piece_recv.at[1], dev(up_h(group // 2), low, j)
    )
    across_copy.start()
    send_x(2)
    across_copy.wait()
    coeffs += across_in[...].astype(jnp.float32)
    gathered[j, mine, :] = coeffs.astype(jnp.bfloat16)
    own = gathered.at[j, mine, :]
    col_copies = {
        (dp, dj): remote(
            own, own, col_send.at[dp, dj], col_recv.at[dp, dj],
            dev((h, pair)[dp], low, up_j(dj)),
        )
        for dp in (1, 0) for dj in turns if (dp, dj) != (0, 0)
    }
    for c in col_copies.values():
        c.start()
    send_x(3)
    for c in limit_copies:
        c.wait()
    lane = lax.broadcasted_iota(jnp.int32, (1, depth), 1)

    def spread(jj):
        number = (jj * samples + lane % samples).astype(jnp.float32)
        for hh in range(group):
            keep = (lane // samples == hh) & (number < limits[hh, 0:1, 0:1])
            left[hh * vectors : (hh + 1) * vectors, aligned(jj * depth, depth)] = (
                gathered[jj] * keep.astype(jnp.bfloat16)
            )

    for dj in range(smp):
        for dp in range(2):
            if (dp, dj) in col_copies:
                col_copies[dp, dj].wait()
        spread((j + smp - dj) % smp)

    for c in tw_copies:
        c.wait()
    o_copies = []
    for k in range(chunks):
        for d, dj in far + [(0, 0)]:
            x_copy(k, d, dj).wait()
        now = slice(starts[k], starts[k] + widths[k])
        product = jnp.dot(left[...], xbuf[:, now], preferred_element_type=jnp.float32)
        field = [product[hh * vectors : (hh + 1) * vectors] for hh in range(group)]
        for level in range(levels):
            distance = group >> (level + 1)
            field = [
                field[hh]
                + twbuf[hh, level : level + 1, now]
                * field[hh ^ distance]
                for hh in range(group)
            ]
        for hh in range(group):
            obuf[hh, :, now] = field[hh].astype(jnp.bfloat16)
        cols = pl.ds(pl.multiple_of(rank * span + starts[k], 128), widths[k])
        for dh, dj in out_order:
            src = obuf.at[up_h(dh), aligned(up_j(dj) * vlocal, vlocal), now]
            dst = out.at[:, cols]
            if (dh, dj) == (0, 0):
                c = pltpu.make_async_copy(src, dst, o_own.at[k])
            else:
                c = remote(
                    src, dst, o_send.at[k, dh, dj], o_recv.at[k, dh, dj],
                    dev(up_h(dh), low, up_j(dj)),
                )
            c.start()
            o_copies.append(c)
    for c in o_copies:
        c.wait()


def body(blocks, smp, fwd, adj, probe, owners, ranks, twiddle):
    samples, box = fwd.shape
    rows, vectors = probe.shape
    levels = twiddle.shape[0]
    group = 2 ** levels
    low_count = blocks // group
    peers = group * smp
    span = box // peers
    widths = tuple(span * w // sum(WIDTHS) for w in WIDTHS)
    chunks = len(widths)
    depth = group * samples
    dma = pltpu.SemaphoreType.DMA
    hbm = pl.BlockSpec(memory_space=pltpu.HBM)
    return pl.pallas_call(
        functools.partial(kernel, blocks, smp, widths),
        out_shape=pltpu.VMEM((vectors // smp, box), jnp.bfloat16),
        in_specs=[
            hbm, hbm, hbm, hbm, hbm,
            pl.BlockSpec(memory_space=pltpu.SMEM),
        ],
        out_specs=pl.BlockSpec(memory_space=pltpu.VMEM),
        scratch_shapes=[
            pltpu.VMEM(adj.shape, jnp.bfloat16),
            pltpu.VMEM((vectors, rows), jnp.bfloat16),
            pltpu.VMEM((1, rows), jnp.int32),
            pltpu.VMEM((low_count, vectors, depth), jnp.float32),
            pltpu.VMEM((low_count, vectors, depth), jnp.bfloat16),
            pltpu.VMEM((low_count, vectors, depth), jnp.bfloat16),
            pltpu.VMEM((vectors // 2, depth), jnp.bfloat16),
            pltpu.VMEM((vectors // 2, depth), jnp.bfloat16),
            pltpu.VMEM((vectors // 2, depth), jnp.bfloat16),
            pltpu.VMEM((vectors // 2, depth), jnp.bfloat16),
            pltpu.VMEM((smp, vectors, depth), jnp.bfloat16),
            pltpu.VMEM((group * vectors, smp * depth), jnp.bfloat16),
            pltpu.VMEM((group, 8, 128), jnp.float32),
            pltpu.VMEM((smp * depth, span), jnp.bfloat16),
            pltpu.VMEM((group, levels, span), jnp.float32),
            pltpu.VMEM((group, vectors, span), jnp.bfloat16),
            pltpu.SemaphoreType.REGULAR,
            dma((3,)),
            dma((low_count,)), dma((low_count,)),
            dma((2,)), dma((2,)),
            dma((2, smp)), dma((2, smp)),
            dma((group,)), dma((group,)),
            dma((chunks, group, smp)), dma((chunks, group, smp)), dma((chunks,)),
            dma((group,)), dma((group,)), dma,
            dma((chunks, group, smp)), dma((chunks, group, smp)), dma((chunks,)),
        ],
        compiler_params=pltpu.CompilerParams(
            collective_id=0, has_side_effects=True, vmem_limit_bytes=66000000
        ),
        name="butterfly",
    )(fwd, adj, probe.T, twiddle, owners.reshape(1, rows), ranks)


def solution(mesh):
    in_specs = (
        P("smp", "blk"),
        P("smp", "blk"),
        P("blk", None),
        P("blk", None),
        P("blk"),
        P(None, "blk"),
    )
    return jax.shard_map(
        functools.partial(body, mesh.shape["blk"], mesh.shape["smp"]),
        mesh=mesh, in_specs=in_specs, out_specs=P("smp", "blk"), check_vma=False,
    )
```

```python
import functools

import jax
import jax.numpy as jnp
from jax import lax
from jax.experimental import pallas as pl
from jax.experimental.pallas import tpu as pltpu
from jax.sharding import PartitionSpec as P

WIDTHS = (2, 2)


def kernel(
    blocks, smp, widths, fwd, adj_in, probe_in, tw_in, owners_in, ranks, out,
    adj, probe, owners, part, part_out, part_in, piece, piece_in, across, across_in, gathered, left, limits,
    xbuf, twbuf, obuf, ready,
    load_sem, part_send, part_recv, piece_send, piece_recv,
    col_send, col_recv, limit_send, limit_recv, x_send, x_recv, x_own,
    tw_send, tw_recv, tw_own, o_send, o_recv, o_own,
):
    levels = tw_in.shape[0]
    group = 2 ** levels
    half_group = group // 2
    low_count = blocks // group
    samples = fwd.shape[0]
    vectors = probe_in.shape[0]
    vlocal = vectors // smp
    span = xbuf.shape[1]
    starts = [sum(widths[:k]) for k in range(len(widths))]
    chunks = len(widths)
    depth = group * samples
    blk, j = lax.axis_index("blk"), lax.axis_index("smp")
    h, low = blk // low_count, blk % low_count
    rank = h * smp + j
    odd = h % 2
    pair = h + 1 - 2 * odd
    inner = ((h + 1) // 2) % 2 == 1

    def up_h(d):
        return (h + d) % group

    def flip(d):
        bits = [(h // 2 ** i) % 2 for i in range(levels)]
        return sum((1 - b if (d >> i) % 2 else b) * 2 ** i for i, b in enumerate(bits))

    def up_j(d):
        return (j + d) % smp

    def dev(hh, ll, jj):
        return {"blk": hh * low_count + ll, "smp": jj}

    def remote(src, dst, send, recv, where):
        return pltpu.make_async_remote_copy(
            src_ref=src, dst_ref=dst, send_sem=send, recv_sem=recv,
            device_id=where, device_id_type=pl.DeviceIdType.MESH,
        )

    shifts = [(dh, dj) for dh in range(group) for dj in range(smp)]
    far = [s for s in shifts if s != (0, 0)]
    far.sort(key=lambda s: (-min(s[0], group - s[0]), s[0], s[1]))
    turns = [*range(smp // 2, smp), *range(smp // 2 - 1, -1, -1)]
    out_order = [
        (d, i) for d in sorted(range(group), key=lambda d: (-min(d, group - d), d)) for i in turns
    ]

    loads = [
        pltpu.make_async_copy(src, dst, load_sem.at[i])
        for i, (src, dst) in enumerate(((owners_in, owners), (adj_in, adj), (probe_in, probe)))
    ]
    barrier = pltpu.get_barrier_semaphore()
    other = [(1 - h // half_group) * half_group + i for i in range(half_group)]
    for hh in other:
        for dj in range(smp):
            pl.semaphore_signal(
                barrier, inc=1, device_id=dev(hh, low, up_j(dj)),
                device_id_type=pl.DeviceIdType.MESH,
            )
    for d in range(1, low_count):
        pl.semaphore_signal(
            barrier, inc=1, device_id=dev(h, (low + d) % low_count, j),
            device_id_type=pl.DeviceIdType.MESH,
        )
    for c in loads:
        c.start()

    def aligned(start, size):
        return pl.ds(pl.multiple_of(start, size), size)

    def x_copy(k, d, dj):
        to = up_h(d) * smp + up_j(dj)
        src = fwd.at[:, pl.ds(pl.multiple_of(to * span + starts[k], 128), widths[k])]
        dst = xbuf.at[
            aligned(j * depth + h * samples, samples), starts[k] : starts[k] + widths[k]
        ]
        if (d, dj) == (0, 0):
            return pltpu.make_async_copy(src, dst, x_own.at[k])
        return remote(
            src, dst, x_send.at[k, d, dj], x_recv.at[k, d, dj], dev(up_h(d), low, up_j(dj))
        )

    plan = (
        [(0, half_group)],
        [(0, group - 1)],
        [(0, d) for d in range(1, group - 1) if d != half_group] + [(0, 0)],
        [
            (k, d)
            for k in range(1, chunks)
            for d in (half_group, 0, *range(1, half_group), *range(half_group + 1, group))
        ],
    )

    def send_x(stage):
        for k, d in plan[stage]:
            for dj in range(smp):
                x_copy(k, d, dj).start()

    def enter():
        pl.semaphore_wait(barrier, half_group * smp + low_count - 1)
        pl.semaphore_signal(
            ready, inc=1, device_id=dev(up_h(half_group), low, j),
            device_id_type=pl.DeviceIdType.MESH,
        )
        send_x(0)

    pl.when(h >= half_group)(enter)
    for c in loads:
        c.wait()

    def partial_sums(lo):
        stacked = jnp.concatenate(
            [
                adj[...] * (owners[...] == hh * low_count + lo).astype(jnp.bfloat16)
                for hh in range(group)
            ],
            axis=0,
        )
        part[lo] = lax.dot_general(
            probe[...], stacked, (((1,), (1,)), ((), ())), preferred_element_type=jnp.float32
        )
        part_out[lo] = part[lo].astype(jnp.bfloat16)

    if low_count > 2:
        lax.fori_loop(0, low_count, lambda lo, c: (partial_sums(lo), c)[1], 0)
    else:
        for lo in range(low_count):
            partial_sums(lo)
    limits[h] = jnp.full(limits.shape[1:], ranks[0].astype(jnp.float32))


    pl.when(h < half_group)(enter)

    def part_copy(d):
        lo = (low + d) % low_count
        return remote(
            part_out.at[lo], part_in.at[d], part_send.at[d], part_recv.at[d], dev(h, lo, j)
        )

    def send_part(d, carry):
        part_copy(d).start()
        return carry

    if low_count > 1:
        lax.fori_loop(1, low_count, send_part, 0)


    total = part.at[low]

    def add_part(d, carry):
        part_copy(d).wait()
        total[...] += part_in[d].astype(jnp.float32)
        return carry

    if low_count > 1:
        lax.fori_loop(1, low_count, add_part, 0)

    half = vectors // 2
    mine, theirs = aligned(odd * half, half), aligned((1 - odd) * half, half)
    piece[...] = total[theirs, :].astype(jnp.bfloat16)
    pair_copy = remote(
        piece, piece_in, piece_send.at[0], piece_recv.at[0], dev(pair, low, j)
    )
    pl.semaphore_wait(ready, 1)
    pair_copy.start()
    tw_copies, limit_copies = [], []
    for dh in range(group):
        src = tw_in.at[:, aligned((up_h(dh) * smp + j) * span, span)]
        dst = twbuf.at[h]
        if dh == 0:
            tw_copies.append(pltpu.make_async_copy(src, dst, tw_own))
        else:
            tw_copies.append(
                remote(src, dst, tw_send.at[dh], tw_recv.at[dh], dev(up_h(dh), low, j))
            )
            limit_copies.append(
                remote(
                    limits.at[h], limits.at[h], limit_send.at[dh], limit_recv.at[dh],
                    dev(up_h(dh), low, j),
                )
            )
    for c in limit_copies + tw_copies:
        c.start()
    send_x(1)
    pair_copy.wait()
    coeffs = total[mine, :] + piece_in[...].astype(jnp.float32)
    across[...] = coeffs.astype(jnp.bfloat16)
    across_copy = remote(
        across, across_in, piece_send.at[1], piece_recv.at[1], dev(up_h(group // 2), low, j)
    )
    across_copy.start()
    send_x(2)
    across_copy.wait()
    coeffs += across_in[...].astype(jnp.float32)
    gathered[j, mine, :] = coeffs.astype(jnp.bfloat16)
    own = gathered.at[j, mine, :]
    col_copies = {
        (dp, dj): remote(
            own, own, col_send.at[dp, dj], col_recv.at[dp, dj],
            dev((h, pair)[dp], low, up_j(dj)),
        )
        for dp in (1, 0) for dj in turns if (dp, dj) != (0, 0)
    }
    for c in col_copies.values():
        c.start()
    send_x(3)
    for c in limit_copies:
        c.wait()
    lane = lax.broadcasted_iota(jnp.int32, (1, depth), 1)

    def spread(jj):
        number = (jj * samples + lane % samples).astype(jnp.float32)
        for hh in range(group):
            keep = (lane // samples == hh) & (number < limits[hh, 0:1, 0:1])
            left[hh * vectors : (hh + 1) * vectors, aligned(jj * depth, depth)] = (
                gathered[jj] * keep.astype(jnp.bfloat16)
            )

    for dj in range(smp):
        for dp in range(2):
            if (dp, dj) in col_copies:
                col_copies[dp, dj].wait()
        spread((j + smp - dj) % smp)

    for c in tw_copies:
        c.wait()
    o_copies = []
    for k in range(chunks):
        for d, dj in far + [(0, 0)]:
            x_copy(k, d, dj).wait()
        now = slice(starts[k], starts[k] + widths[k])
        product = jnp.dot(left[...], xbuf[:, now], preferred_element_type=jnp.float32)
        field = [product[hh * vectors : (hh + 1) * vectors] for hh in range(group)]
        for level in range(levels):
            distance = group >> (level + 1)
            field = [
                field[hh]
                + twbuf[hh, level : level + 1, now]
                * field[hh ^ distance]
                for hh in range(group)
            ]
        for hh in range(group):
            obuf[hh, :, now] = field[hh].astype(jnp.bfloat16)
        cols = pl.ds(pl.multiple_of(rank * span + starts[k], 128), widths[k])
        for dh, dj in out_order:
            src = obuf.at[up_h(dh), aligned(up_j(dj) * vlocal, vlocal), now]
            dst = out.at[:, cols]
            if (dh, dj) == (0, 0):
                c = pltpu.make_async_copy(src, dst, o_own.at[k])
            else:
                c = remote(
                    src, dst, o_send.at[k, dh, dj], o_recv.at[k, dh, dj],
                    dev(up_h(dh), low, up_j(dj)),
                )
            c.start()
            o_copies.append(c)
    for c in o_copies:
        c.wait()


def body(blocks, smp, fwd, adj, probe, owners, ranks, twiddle):
    samples, box = fwd.shape
    rows, vectors = probe.shape
    levels = twiddle.shape[0]
    group = 2 ** levels
    low_count = blocks // group
    peers = group * smp
    span = box // peers
    widths = tuple(span * w // sum(WIDTHS) for w in WIDTHS)
    chunks = len(widths)
    depth = group * samples
    dma = pltpu.SemaphoreType.DMA
    hbm = pl.BlockSpec(memory_space=pltpu.HBM)
    return pl.pallas_call(
        functools.partial(kernel, blocks, smp, widths),
        out_shape=pltpu.VMEM((vectors // smp, box), jnp.bfloat16),
        in_specs=[
            hbm, hbm, hbm, hbm, hbm,
            pl.BlockSpec(memory_space=pltpu.SMEM),
        ],
        out_specs=pl.BlockSpec(memory_space=pltpu.VMEM),
        scratch_shapes=[
            pltpu.VMEM(adj.shape, jnp.bfloat16),
            pltpu.VMEM((vectors, rows), jnp.bfloat16),
            pltpu.VMEM((1, rows), jnp.int32),
            pltpu.VMEM((low_count, vectors, depth), jnp.float32),
            pltpu.VMEM((low_count, vectors, depth), jnp.bfloat16),
            pltpu.VMEM((low_count, vectors, depth), jnp.bfloat16),
            pltpu.VMEM((vectors // 2, depth), jnp.bfloat16),
            pltpu.VMEM((vectors // 2, depth), jnp.bfloat16),
            pltpu.VMEM((vectors // 2, depth), jnp.bfloat16),
            pltpu.VMEM((vectors // 2, depth), jnp.bfloat16),
            pltpu.VMEM((smp, vectors, depth), jnp.bfloat16),
            pltpu.VMEM((group * vectors, smp * depth), jnp.bfloat16),
            pltpu.VMEM((group, 8, 128), jnp.float32),
            pltpu.VMEM((smp * depth, span), jnp.bfloat16),
            pltpu.VMEM((group, levels, span), jnp.float32),
            pltpu.VMEM((group, vectors, span), jnp.bfloat16),
            pltpu.SemaphoreType.REGULAR,
            dma((3,)),
            dma((low_count,)), dma((low_count,)),
            dma((2,)), dma((2,)),
            dma((2, smp)), dma((2, smp)),
            dma((group,)), dma((group,)),
            dma((chunks, group, smp)), dma((chunks, group, smp)), dma((chunks,)),
            dma((group,)), dma((group,)), dma,
            dma((chunks, group, smp)), dma((chunks, group, smp)), dma((chunks,)),
        ],
        compiler_params=pltpu.CompilerParams(
            collective_id=0, has_side_effects=True, vmem_limit_bytes=66000000
        ),
        name="butterfly",
    )(fwd, adj, probe.T, twiddle, owners.reshape(1, rows), ranks)


def solution(mesh):
    in_specs = (
        P("smp", "blk"),
        P("smp", "blk"),
        P("blk", None),
        P("blk", None),
        P("blk"),
        P(None, "blk"),
    )
    return jax.shard_map(
        functools.partial(body, mesh.shape["blk"], mesh.shape["smp"]),
        mesh=mesh, in_specs=in_specs, out_specs=P("smp", "blk"), check_vma=False,
    )
```
